32 devices in a mesh: grp: 4 (over y, x), wide: 8 (over z, core).
Axes of the slice: x: 2, y: 2, z: 4, core: 2. Of those that a mesh axis runs over, the one named last changes fastest.
Arguments:
- features: bfloat16 [32768, 512], P(('grp', 'wide')), may hold values from -6 to 6
- positions: float32 [3, 32768], P(None, ('grp', 'wide')), may hold values from 0 to 1
- lattice: int32 [3, 2048], replicated, may hold values from -12 to 12
- kernel: float32 [2048, 512], replicated, may hold values from -5 to 5
Outputs:
- updated: bfloat16 [32768, 512], P(('grp', 'wide'))
The draws below stay inside these ranges and needn't reach their ends.
All inputs are finite; a program needn't handle non-finite values.
Results may differ from the reference program's by a relative error of at most 0.0046.
Values may be sent and summed in bfloat16 or wider, within the bound.
No kernel may reach another device: no remote copies, remote signals or barrier semaphores. Data moves between devices by JAX's collectives and lax.ppermute only.
A program may use at most 64 MiB of HBM per device.

```python
import math
import jax
import jax.numpy as jnp
from jax import lax

D = 512
K = 2048
ATOMS = 32768


def plant(result, stream_key, smallest, largest):
    longest = result.shape.index(max(result.shape))
    spots = []
    for shift in (0, 1):
        where = [jax.random.randint(jax.random.fold_in(stream_key, axis), (), 0, length) for axis, length in enumerate(result.shape)]
        where[longest] = (where[longest] + shift) % result.shape[longest]
        spots.append(tuple(where))
    return result.at[spots[0]].set(smallest).at[spots[1]].set(largest)


def levels(own_key, shape, pieces, least, top_value):
    def one(dim, parts):
        draws = jax.random.uniform(jax.random.fold_in(jax.random.fold_in(own_key, 6), dim), (parts,), jnp.float32, least / len(pieces), top_value / len(pieces))
        return jnp.repeat(jnp.exp(draws), shape[dim] // parts).reshape((-1,) + (1,) * (len(shape) - dim - 1))

    factor_of = one(*pieces[0])
    for cut in pieces[1:]:
        factor_of = factor_of * one(*cut)
    return factor_of


def bell_draw(own_key, dims, width, most, pieces=(), kind=jnp.bfloat16):
    result = jax.random.normal(own_key, dims, jnp.float32) * width
    if len(pieces) > 0:
        result = levels(own_key, dims, pieces, -0.22, 0.18) * result
    return jnp.clip(result, min=-most, max=most).astype(kind)


def setup_inputs(seed: int = 0) -> dict:
    key_of = jax.random.split(jax.random.key(seed), 5)
    return {
        "features": bell_draw(key_of[0], (ATOMS, D), 1.0, 6.0, ((0, 32),)),
        "positions": jnp.clip(1.0 * jax.random.uniform(key_of[1], (3, ATOMS), jnp.float32) ** levels(key_of[1], (3, ATOMS), ((1, 32),), -0.2, 0.2), 0.0, 1.0),
        "lattice": plant(jax.random.randint(key_of[2], (3, K), -12, 13), jax.random.fold_in(key_of[2], 1), -12, 12).astype(jnp.int32),
        "kernel": bell_draw(key_of[3], (K, D), 1.0, 5.0, (), jnp.float32),
    }


two_pi = 6.283185307179586

def phase_tables(block_pos, lattice):
    grid = lattice.astype(jnp.float32)
    inner = block_pos[0][:, None] * grid[0][None, :] + block_pos[1][:, None] * grid[1][None, :]
    inner = inner + block_pos[2][:, None] * grid[2][None, :]
    angle = two_pi * inner
    return (jnp.cos(angle).astype(jnp.bfloat16), jnp.sin(angle).astype(jnp.bfloat16))

def reference(features, positions, lattice, kernel):
    block = math.gcd(ATOMS, 2048)
    count = ATOMS // block
    feat_blocks = features.reshape(count, block, D)
    pos_blocks = positions.reshape(3, count, block).transpose(1, 0, 2)

    def accumulate(total, item):
        block_pos, block_feat = item
        cosines, sines = phase_tables(block_pos, lattice)
        part_cos = jnp.dot(cosines.T, block_feat, preferred_element_type=jnp.float32)
        part_sin = jnp.dot(sines.T, block_feat, preferred_element_type=jnp.float32)
        return (total + jnp.concatenate([part_cos, part_sin], axis=1), None)
    start = jnp.zeros((K, 2 * D), jnp.float32)
    factors, unused = lax.scan(accumulate, start, (pos_blocks, feat_blocks))
    factors = factors / jnp.sqrt(jnp.float32(ATOMS))
    filtered = (factors * jnp.concatenate([kernel, kernel], axis=1)).astype(jnp.bfloat16)

    def message(item):
        block_pos, block_feat = item
        cosines, sines = phase_tables(block_pos, lattice)
        summed = jnp.dot(cosines, filtered[:, :D], preferred_element_type=jnp.float32)
        summed = summed + jnp.dot(sines, filtered[:, D:], preferred_element_type=jnp.float32)
        summed = summed / jnp.sqrt(jnp.float32(K))
        return (block_feat.astype(jnp.float32) + summed).astype(jnp.bfloat16)
    updated = lax.map(message, (pos_blocks, feat_blocks))
    return updated.reshape(ATOMS, D)
```

```python
import functools
import jax
import jax.numpy as jnp
from jax import lax
from jax.experimental import pallas as pl
from jax.experimental.pallas import tpu as pltpu
from jax.sharding import PartitionSpec as P


AXES = ("grp", "wide")
CHUNKS = 2
MAGIC = 12582912.0
SIN = (4.4428679, -7.30744342, 3.59478806, -0.78437397)
COS = (1.4142135, -6.97885099, 5.73946117, -1.88356297, 0.31069815)
TILE = 256


def turns_to_tables(turns):
    rest = turns - ((turns + MAGIC) - MAGIC)
    square = rest * rest
    half_sin = rest * (SIN[0] + square * (SIN[1] + square * (SIN[2] + square * SIN[3])))
    half_cos = COS[3] + square * COS[4]
    for term in (COS[2], COS[1], COS[0]):
        half_cos = term + square * half_cos
    return 1.0 - half_sin * half_sin, half_sin * half_cos


def stage_orders(groups, wides):
    grp_bits = [("grp", b) for b in range(groups.bit_length() - 1)]
    wide_bits = [("wide", b) for b in range(1, wides.bit_length() - 1)]
    return (grp_bits + wide_bits, grp_bits[::-1] + wide_bits[::-1])


def flip(g, w, where):
    axis, bit = where
    return (g ^ (1 << bit), w) if axis == "grp" else (g, w ^ (1 << bit))


def stage_bit(orders, j):
    def one(where):
        return (lax.axis_index(where[0]) >> where[1]) & 1

    core = lax.axis_index("wide") & 1
    return one(orders[0][j]) * (1 - core) + one(orders[1][j]) * core


def blend(bit, zero, one):
    share = bit.astype(jnp.float32)
    return zero + share * (one - zero)


def factor_kernel(orders, chunk, half, waves, lat_ref, own_pos, mate_pos, own_feat, mate_feat, cos_ref, sin_ref, part_ref):
    stages = len(orders[0])
    side = lat_ref.shape[1] // 2
    core = lax.axis_index("wide") & 1
    at = chunk * waves
    mine = blend(core, lat_ref[:, at:at + waves], lat_ref[:, side + at:side + at + waves])
    wide = waves // 2
    top = stage_bit(orders, 0)
    top = top if half == 0 else 1 - top
    grid = blend(top, mine[:, :wide], mine[:, wide:])
    lane = lax.broadcasted_iota(jnp.int32, grid.shape, 1)
    for j in range(1, stages):
        step = waves >> (j + 1)
        low = (lane & step) == 0
        swapped = jnp.where(low, pltpu.roll(grid, wide - step, 1), pltpu.roll(grid, step, 1))
        grid = blend(stage_bit(orders, j), grid, swapped)
    grid = grid.astype(jnp.bfloat16)
    rows = own_feat.shape[0]
    tile = min(TILE, rows)
    for first, pos_ref in ((0, own_pos), (rows, mate_pos)):
        def fill(t, unused, first=first, pos_ref=pos_ref):
            start = pl.multiple_of(t * tile, tile)
            turns = lax.dot_general(pos_ref[:, pl.ds(start, tile)], grid, (((0,), (0,)), ((), ())), preferred_element_type=jnp.float32)
            for r in range(0, tile, 32):
                c, s = turns_to_tables(turns[r:r + 32])
                cos_ref[pl.ds(first + start + r, 32), :] = c.astype(jnp.bfloat16)
                sin_ref[pl.ds(first + start + r, 32), :] = s.astype(jnp.bfloat16)
            return unused

        lax.fori_loop(0, rows // tile, fill, 0)
    depth = own_feat.shape[1]
    for n, table in ((0, cos_ref), (1, sin_ref)):
        total = lax.dot_general(table[:rows], own_feat[...], (((0,), (0,)), ((), ())), preferred_element_type=jnp.float32)
        total += lax.dot_general(table[rows:], mate_feat[...], (((0,), (0,)), ((), ())), preferred_element_type=jnp.float32)
        part_ref[:, n * depth:(n + 1) * depth] = total.astype(part_ref.dtype)


def factor_part(orders, chunk, half, waves, lat, own_pos, mate_pos, own_feat, mate_feat):
    rows, depth = own_feat.shape
    wide = waves // 2
    table = jax.ShapeDtypeStruct((2 * rows, wide), jnp.bfloat16)
    part = jax.ShapeDtypeStruct((wide, 2 * depth), jnp.bfloat16 if half == 0 else jnp.float32)
    return pl.pallas_call(
        functools.partial(factor_kernel, orders, chunk, half, waves),
        out_shape=(table, table, part),
        compiler_params=pltpu.CompilerParams(vmem_limit_bytes=40 << 20),
        cost_estimate=pl.CostEstimate(flops=8 * rows * wide * depth, bytes_accessed=12 << 20, transcendentals=0),
        name=f"factor_{chunk}_{half}",
    )(lat, own_pos, mate_pos, own_feat, mate_feat)


def message_kernel(pieces, has_base, scale, *refs):
    refs = list(refs)
    out_ref = refs.pop()
    depth = out_ref.shape[1]
    total = refs.pop()[...] if has_base else None
    for n in range(pieces):
        cos_ref, sin_ref, filt_ref = refs[3 * n:3 * n + 3]
        for table, at in ((cos_ref, 0), (sin_ref, depth)):
            more = jnp.dot(table[...], filt_ref[:, at:at + depth], preferred_element_type=jnp.float32)
            total = more if total is None else total + more
    out_ref[...] = (total * scale).astype(out_ref.dtype)


def message_part(pieces, base, first, rows, scale, kind, name):
    tile = min(TILE, rows)
    ahead = first // tile
    depth = pieces[0][2].shape[1] // 2
    specs, args = [], []
    for cos, sin, filt in pieces:
        table = pl.BlockSpec((tile, cos.shape[1]), lambda i: (i + ahead, 0))
        specs += [table, table, pl.BlockSpec(filt.shape, lambda i: (0, 0))]
        args += [cos, sin, filt]
    if base is not None:
        specs.append(pl.BlockSpec((tile, depth), lambda i: (i + ahead, 0)))
        args.append(base)
    waves = sum(p[2].shape[0] for p in pieces)
    return pl.pallas_call(
        functools.partial(message_kernel, len(pieces), base is not None, scale),
        grid=(rows // tile,),
        in_specs=specs,
        out_specs=pl.BlockSpec((tile, depth), lambda i: (i, 0)),
        out_shape=jax.ShapeDtypeStruct((rows, depth), kind),
        cost_estimate=pl.CostEstimate(flops=4 * rows * waves * depth, bytes_accessed=rows * (4 * waves + 4 * depth), transcendentals=0),
        name=name,
    )(*args)


def make_body(groups, wides):
    orders = stage_orders(groups, wides)
    stages = len(orders[0])
    spots = [(g, w) for g in range(groups) for w in range(wides)]

    def pairs(target):
        out = []
        for g, w in spots:
            tg, tw = target(g, w)
            out.append((g * wides + w, tg * wides + tw))
        return out

    mate = pairs(lambda g, w: (g, w ^ 1))
    hops = [pairs(lambda g, w, j=j: flip(g, w, orders[w & 1][j])) for j in range(stages)]

    def body(features, positions, lattice, kernel):
        waves_all, depth = kernel.shape
        rows = features.shape[0]
        atoms = rows * groups * wides
        inv_atoms = 1.0 / jnp.sqrt(jnp.float32(atoms))
        inv_waves = float(1.0 / waves_all ** 0.5)
        waves = waves_all // (2 * CHUNKS)
        core = lax.axis_index("wide") & 1

        high = lax.reduce_precision(positions, 8, 7)
        rest = positions - high
        mid = lax.reduce_precision(rest, 8, 7)
        low = rest - mid
        own_pos = jnp.concatenate([high, mid, low, jnp.zeros((7, rows), jnp.float32)], 0).astype(jnp.bfloat16)
        mate_pos = lax.ppermute(own_pos, AXES, mate)
        mate_feat = lax.ppermute(features, AXES, mate)
        lat = lattice.astype(jnp.float32)
        lat = jnp.concatenate([lat, lat, lat, jnp.zeros((7, waves_all), jnp.float32)], 0)

        block = waves >> stages
        mask = sum(stage_bit(orders, j) << (stages - 1 - j) for j in range(stages))
        spot = ((1 << stages) - 1) ^ mask
        filters = []
        for c in range(CHUNKS):
            at = core * (waves_all // 2) + c * waves + spot * block
            filters.append(lax.dynamic_slice_in_dim(kernel, at, block, 0) * inv_atoms)

        tables, sends, keeps = [], [], []
        for c in range(CHUNKS):
            a = factor_part(orders, c, 0, waves, lat, own_pos, mate_pos, features, mate_feat)
            b = factor_part(orders, c, 1, waves, lat, own_pos, mate_pos, features, mate_feat)
            tables.append(((a[0], a[1]), (b[0], b[1])))
            sends.append(a[2])
            keeps.append(b[2])

        mine = []
        for c in range(CHUNKS):
            send, keep = sends[c], keeps[c]
            for j in range(stages):
                got = lax.ppermute(send, AXES, hops[j])
                keep = keep + got.astype(jnp.float32)
                if j < stages - 1:
                    half = keep.shape[0] // 2
                    send = keep[:half].astype(jnp.bfloat16)
                    keep = keep[half:]
            scale = filters[c]
            mine.append((keep * jnp.concatenate([scale, scale], 1)).astype(jnp.bfloat16))

        lasts = []
        for c in range(CHUNKS):
            piece = mine[c]
            for j in range(stages - 1, 0, -1):
                got = lax.ppermute(piece, AXES, hops[j])
                piece = jnp.concatenate([got, piece], 0)
            lasts.append((lax.ppermute(piece, AXES, hops[0]), piece))

        early = []
        for c in range(CHUNKS):
            if c < CHUNKS - 1:
                early.append((*tables[c][0], lasts[c][0]))
            early.append((*tables[c][1], lasts[c][1]))
        late = [(*tables[-1][0], lasts[-1][0])]
        base = message_part(early, None, 0, 2 * rows, 1.0, jnp.float32, "message_early")
        away = message_part(late, base, rows, rows, inv_waves, jnp.bfloat16, "message_mate")
        back = lax.ppermute(away, AXES, mate)
        home = message_part(late, base, 0, rows, inv_waves, jnp.float32, "message_own")
        return (features.astype(jnp.float32) + (home + back.astype(jnp.float32))).astype(jnp.bfloat16)

    return body


def solution(mesh):
    placed = (P(AXES, None), P(None, AXES), P(), P())
    return jax.shard_map(
        make_body(mesh.shape["grp"], mesh.shape["wide"]),
        mesh=mesh,
        in_specs=placed,
        out_specs=P(AXES, None),
        check_vma=False,
    )
```

```python
import functools
import jax
import jax.numpy as jnp
from jax import lax
from jax.experimental import pallas as pl
from jax.experimental.pallas import tpu as pltpu
from jax.sharding import PartitionSpec as P


AXES = ("grp", "wide")
CHUNKS = 2
MAGIC = 12582912.0
SIN = (4.4428679, -7.30744342, 3.59478806, -0.78437397)
COS = (1.4142135, -6.97885099, 5.73946117, -1.88356297, 0.31069815)
TILE = 256


def turns_to_tables(turns):
    rest = turns - ((turns + MAGIC) - MAGIC)
    square = rest * rest
    half_sin = rest * (SIN[0] + square * (SIN[1] + square * (SIN[2] + square * SIN[3])))
    half_cos = COS[3] + square * COS[4]
    for term in (COS[2], COS[1], COS[0]):
        half_cos = term + square * half_cos
    return 1.0 - half_sin * half_sin, half_sin * half_cos


def stage_orders(groups):
    bits = list(range(groups.bit_length() - 1))
    return bits, bits[::-1]


def stage_bit(orders, j):
    core = lax.axis_index("wide") & 1
    group = lax.axis_index("grp")
    return ((group >> orders[0][j]) & 1) * (1 - core) + ((group >> orders[1][j]) & 1) * core


def blend(bit, zero, one):
    share = bit.astype(jnp.float32)
    return zero + share * (one - zero)


def factor_kernel(orders, lines, chunk, half, waves, lat_ref, own_pos, mate_pos, own_feat, mate_feat, cos_ref, sin_ref, part_ref):
    stages = len(orders[0])
    lat = lat_ref[...].astype(jnp.float32)
    side = lat.shape[1] // 2
    core = lax.axis_index("wide") & 1
    at = chunk * waves
    mine = blend(core, lat[:, at:at + waves], lat[:, side + at:side + at + waves])
    bits = [stage_bit(orders, j) for j in range(stages)]
    line = lax.axis_index("wide") >> 1
    for b in reversed(range(lines.bit_length() - 1)):
        bits.append((line >> b) & 1)
    wide = waves // 2
    top = bits[0] if half == 0 else 1 - bits[0]
    grid = blend(top, mine[:, :wide], mine[:, wide:])
    lane = lax.broadcasted_iota(jnp.int32, grid.shape, 1)
    for j in range(1, len(bits)):
        step = waves >> (j + 1)
        low = (lane & step) == 0
        swapped = jnp.where(low, pltpu.roll(grid, wide - step, 1), pltpu.roll(grid, step, 1))
        grid = blend(bits[j], grid, swapped)
    grid = grid.astype(jnp.bfloat16)
    rows = own_feat.shape[0]
    tile = min(TILE, rows)
    for first, pos_ref in ((0, own_pos), (rows, mate_pos)):
        def fill(t, unused, first=first, pos_ref=pos_ref):
            start = pl.multiple_of(t * tile, tile)
            pos = pos_ref[:, pl.ds(start, tile)]
            turns = None
            for _ in range(3):
                level = pos.astype(jnp.bfloat16)
                more = lax.dot_general(level, grid, (((0,), (0,)), ((), ())), preferred_element_type=jnp.float32)
                turns = more if turns is None else turns + more
                pos = pos - level.astype(jnp.float32)
            for r in range(0, tile, 32):
                c, s = turns_to_tables(turns[r:r + 32])
                cos_ref[pl.ds(first + start + r, 32), :] = c.astype(jnp.bfloat16)
                sin_ref[pl.ds(first + start + r, 32), :] = s.astype(jnp.bfloat16)
            return unused

        lax.fori_loop(0, rows // tile, fill, 0)
    depth = own_feat.shape[1]
    for n, table in ((0, cos_ref), (1, sin_ref)):
        total = lax.dot_general(table[:rows], own_feat[...], (((0,), (0,)), ((), ())), preferred_element_type=jnp.float32)
        total += lax.dot_general(table[rows:], mate_feat[...], (((0,), (0,)), ((), ())), preferred_element_type=jnp.float32)
        part_ref[:, n * depth:(n + 1) * depth] = total.astype(part_ref.dtype)


def factor_part(orders, lines, chunk, half, waves, lat, own_pos, mate_pos, own_feat, mate_feat):
    rows, depth = own_feat.shape
    wide = waves // 2
    table = jax.ShapeDtypeStruct((2 * rows, wide), jnp.bfloat16)
    part = jax.ShapeDtypeStruct((wide, 2 * depth), jnp.bfloat16 if half == 0 else jnp.float32)
    return pl.pallas_call(
        functools.partial(factor_kernel, orders, lines, chunk, half, waves),
        out_shape=(table, table, part),
        compiler_params=pltpu.CompilerParams(vmem_limit_bytes=16 << 20),
        cost_estimate=pl.CostEstimate(flops=8 * rows * wide * depth, bytes_accessed=12 << 20, transcendentals=0),
        name=f"factor_{chunk}_{half}",
    )(lat, own_pos, mate_pos, own_feat, mate_feat)


def message_kernel(pieces, has_base, first, scale, *refs):
    refs = list(refs)
    out_ref = refs.pop()
    base_ref = refs.pop() if has_base else None
    rows, depth = out_ref.shape
    tile = min(TILE, rows)
    behind = first if has_base else 0

    def step(t, unused):
        start = pl.multiple_of(t * tile, tile)
        total = base_ref[pl.ds(behind + start, tile), :] if has_base else None
        for n in range(pieces):
            cos_ref, sin_ref, filt_ref = refs[3 * n:3 * n + 3]
            for table, at in ((cos_ref, 0), (sin_ref, depth)):
                more = jnp.dot(table[pl.ds(first + start, tile), :], filt_ref[:, at:at + depth], preferred_element_type=jnp.float32)
                total = more if total is None else total + more
        out_ref[pl.ds(start, tile), :] = (total * scale).astype(out_ref.dtype)
        return unused

    lax.fori_loop(0, rows // tile, step, 0)


def message_part(pieces, base, first, rows, scale, kind, name):
    depth = pieces[0][2].shape[1] // 2
    args = [x for piece in pieces for x in piece]
    if base is not None:
        args.append(base)
    waves = sum(p[2].shape[0] for p in pieces)
    return pl.pallas_call(
        functools.partial(message_kernel, len(pieces), base is not None, first, scale),
        out_shape=jax.ShapeDtypeStruct((rows, depth), kind),
        compiler_params=pltpu.CompilerParams(vmem_limit_bytes=8 << 20),
        cost_estimate=pl.CostEstimate(flops=4 * rows * waves * depth, bytes_accessed=rows * (4 * waves + 4 * depth), transcendentals=0),
        name=name,
    )(*args)


def make_body(groups, wides):
    orders = stage_orders(groups)
    stages = len(orders[0])
    lines = wides // 2
    spots = [(g, w) for g in range(groups) for w in range(wides)]

    def pairs(target):
        out = []
        for g, w in spots:
            tg, tw = target(g, w)
            out.append((g * wides + w, tg * wides + tw))
        return out

    mate = pairs(lambda g, w: (g, w ^ 1))
    hops = [pairs(lambda g, w, j=j: (g ^ (1 << orders[w & 1][j]), w)) for j in range(stages)]
    along = [pairs(lambda g, w, d=d: (g, w ^ (2 * d))) for d in range(lines)]

    def body(features, positions, lattice, kernel):
        waves_all, depth = kernel.shape
        rows = features.shape[0]
        atoms = rows * groups * wides
        inv_atoms = 1.0 / jnp.sqrt(jnp.float32(atoms))
        inv_waves = float(1.0 / waves_all ** 0.5)
        waves = waves_all // (2 * CHUNKS)
        core = lax.axis_index("wide") & 1

        mate_pos = lax.ppermute(positions, AXES, mate)
        mate_feat = lax.ppermute(features, AXES, mate)

        block = waves // (groups * lines)
        spot = lax.axis_index("wide") >> 1
        for j in range(stages):
            spot += (1 - stage_bit(orders, j)) * (lines << (stages - 1 - j))
        filters = []
        for c in range(CHUNKS):
            at = core * (waves_all // 2) + c * waves + spot * block
            filters.append(lax.dynamic_slice_in_dim(kernel, at, block, 0) * inv_atoms)

        tables, sends, keeps = [], [], []
        for c in range(CHUNKS):
            a, b = (factor_part(orders, lines, c, h, waves, lattice, positions, mate_pos, features, mate_feat) for h in (0, 1))
            tables.append(((a[0], a[1]), (b[0], b[1])))
            sends.append(a[2])
            keeps.append(b[2])

        mine = []
        for c in range(CHUNKS):
            send, keep = sends[c], keeps[c]
            for j in range(stages):
                got = lax.ppermute(send, AXES, hops[j])
                keep = keep + got.astype(jnp.float32)
                if j < stages - 1:
                    half = keep.shape[0] // 2
                    send = keep[:half].astype(jnp.bfloat16)
                    keep = keep[half:]
            total = keep[:block]
            outs = [keep[d * block:(d + 1) * block].astype(jnp.bfloat16) for d in range(1, lines)]
            for d in range(1, lines):
                total = total + lax.ppermute(outs[d - 1], AXES, along[d]).astype(jnp.float32)
            scale = filters[c]
            mine.append((total * jnp.concatenate([scale, scale], 1)).astype(jnp.bfloat16))

        lasts = []
        for c in range(CHUNKS):
            piece = jnp.concatenate([mine[c]] + [lax.ppermute(mine[c], AXES, along[d]) for d in range(1, lines)], 0)
            for j in range(stages - 1, 0, -1):
                got = lax.ppermute(piece, AXES, hops[j])
                piece = jnp.concatenate([got, piece], 0)
            lasts.append((lax.ppermute(piece, AXES, hops[0]), piece))

        base = None
        for c in range(CHUNKS):
            pieces = [(*tables[c][1], lasts[c][1])]
            if c < CHUNKS - 1:
                pieces.append((*tables[c][0], lasts[c][0]))
            base = message_part(pieces, base, 0, 2 * rows, 1.0, jnp.float32, f"message_{c}")
        late = [(*tables[-1][0], lasts[-1][0])]
        away = message_part(late, base, rows, rows, inv_waves, jnp.bfloat16, "message_mate")
        back = lax.ppermute(away, AXES, mate)
        home = message_part(late, base, 0, rows, inv_waves, jnp.float32, "message_own")
        return (features.astype(jnp.float32) + (home + back.astype(jnp.float32))).astype(jnp.bfloat16)

    return body


def solution(mesh):
    placed = (P(AXES, None), P(None, AXES), P(), P())
    return jax.shard_map(
        make_body(mesh.shape["grp"], mesh.shape["wide"]),
        mesh=mesh,
        in_specs=placed,
        out_specs=P(AXES, None),
        check_vma=False,
    )
```

```python
import functools
import jax
import jax.numpy as jnp
from jax import lax
from jax.experimental import pallas as pl
from jax.experimental.pallas import tpu as pltpu
from jax.sharding import PartitionSpec as P


AXES = ("grp", "wide")
CHUNKS = 2
MAGIC = 12582912.0
SIN = (4.4428679, -7.30744342, 3.59478806, -0.78437397)
COS = (1.41420408, -6.97764204, 5.71523826, -1.72834831)
TILE = 256


def turns_to_tables(turns):
    rest = turns - ((turns + MAGIC) - MAGIC)
    square = rest * rest
    half_sin = rest * (SIN[0] + square * (SIN[1] + square * (SIN[2] + square * SIN[3])))
    half_cos = COS[0] + square * (COS[1] + square * (COS[2] + square * COS[3]))
    return 1.0 - half_sin * half_sin, half_sin * half_cos


def stage_orders(groups):
    bits = list(range(groups.bit_length() - 1))
    return bits, bits[::-1]


def stage_bit(orders, j):
    core = lax.axis_index("wide") & 1
    group = lax.axis_index("grp")
    return ((group >> orders[0][j]) & 1) * (1 - core) + ((group >> orders[1][j]) & 1) * core


def blend(bit, zero, one):
    share = bit.astype(jnp.float32)
    return zero + share * (one - zero)


def padded(ref, wide_ref):
    wide_ref[...] = jnp.zeros_like(wide_ref)
    wide_ref[0:ref.shape[0], :] = ref[...].astype(jnp.float32)
    return wide_ref[...]


def levels(pos):
    parts = []
    for _ in range(3):
        part = pos.astype(jnp.bfloat16).astype(jnp.float32)
        pos = pos - part
        parts.append(part)
    return jnp.concatenate(parts + [jnp.zeros_like(pos)], 0).astype(jnp.bfloat16)


def fill_tables(grid, pos_ref, cos_ref, sin_ref):
    rows = cos_ref.shape[0]
    tile = min(TILE, rows)

    def fill(t, unused):
        start = pl.multiple_of(t * tile, tile)
        turns = lax.dot_general(pos_ref[:, pl.ds(start, tile)], grid, (((0,), (0,)), ((), ())), preferred_element_type=jnp.float32)
        for r in range(0, tile, 32):
            c, s = turns_to_tables(turns[r:r + 32])
            cos_ref[pl.ds(start + r, 32), :] = c.astype(jnp.bfloat16)
            sin_ref[pl.ds(start + r, 32), :] = s.astype(jnp.bfloat16)
        return unused

    lax.fori_loop(0, rows // tile, fill, 0)


def filter_row(orders, lines, waves_all, waves, chunk):
    stages = len(orders[0])
    spot = lax.axis_index("wide") >> 1
    for j in range(stages):
        spot += (1 - stage_bit(orders, j)) * (lines << (stages - 1 - j))
    block = waves // (lines << stages)
    return (lax.axis_index("wide") & 1) * (waves_all // 2) + chunk * waves + spot * block, block


def first_kernel(orders, lines, waves, lat_hbm, pos_hbm, kern_hbm, grid_ref, own_ref, cos_ref, sin_ref, filt_ref, lat_ref, pos_ref, lat_wide, pos_wide, sems):
    pairs = ((lat_hbm, lat_ref), (pos_hbm, pos_ref))
    copies = [pltpu.make_async_copy(a, b, sems.at[n]) for n, (a, b) in enumerate(pairs)]
    for copy in copies:
        copy.start()
    slices = []
    for c in range(filt_ref.shape[0]):
        at, block = filter_row(orders, lines, kern_hbm.shape[0], waves, c)
        if block % 8 == 0:
            at = pl.multiple_of(at, block)
            slices.append(pltpu.make_async_copy(kern_hbm.at[pl.ds(at, block), :], filt_ref.at[c], sems.at[2 + c]))
            slices[-1].start()
    for copy in copies:
        copy.wait()
    lat = padded(lat_ref, lat_wide)
    side = lat.shape[1] // 2
    core = lax.axis_index("wide") & 1
    grid = blend(core, lat[:, :side], lat[:, side:])
    bits = [stage_bit(orders, j) for j in range(len(orders[0]))]
    line = lax.axis_index("wide") >> 1
    for b in reversed(range(lines.bit_length() - 1)):
        bits.append((line >> b) & 1)
    lane = lax.broadcasted_iota(jnp.int32, grid.shape, 1)
    for j, bit in enumerate(bits):
        step = waves >> (j + 1)
        low = (lane & step) == 0
        swapped = jnp.where(low, pltpu.roll(grid, side - step, 1), pltpu.roll(grid, step, 1))
        grid = blend(bit, grid, swapped)
    grid_ref[...] = jnp.concatenate([grid, grid, grid, jnp.zeros_like(grid)], 0).astype(jnp.bfloat16)
    own_ref[...] = levels(padded(pos_ref, pos_wide))
    fill_tables(grid_ref[:, :waves // 2], own_ref, cos_ref, sin_ref)
    for copy in slices:
        copy.wait()


def table_of(rows, waves):
    return jax.ShapeDtypeStruct((rows, waves // 2), jnp.bfloat16)


def first_part(orders, lines, waves, lat, pos, kern):
    rows = pos.shape[1]
    block = waves // (lines << len(orders[0]))
    return pl.pallas_call(
        functools.partial(first_kernel, orders, lines, waves),
        in_specs=[pl.BlockSpec(memory_space=pltpu.HBM)] * 3,
        out_shape=(
            jax.ShapeDtypeStruct((32, lat.shape[1] // 2), jnp.bfloat16),
            jax.ShapeDtypeStruct((32, rows), jnp.bfloat16),
            table_of(rows, waves),
            table_of(rows, waves),
            jax.ShapeDtypeStruct((CHUNKS, block, kern.shape[1]), jnp.float32),
        ),
        scratch_shapes=[
            pltpu.VMEM(lat.shape, lat.dtype),
            pltpu.VMEM(pos.shape, pos.dtype),
            pltpu.VMEM((8, lat.shape[1]), jnp.float32),
            pltpu.VMEM((8, rows), jnp.float32),
            pltpu.SemaphoreType.DMA((2 + CHUNKS,)),
        ],
        compiler_params=pltpu.CompilerParams(vmem_limit_bytes=12 << 20),
        cost_estimate=pl.CostEstimate(flops=rows * waves * 600, bytes_accessed=1 << 20, transcendentals=0),
        name="factor_first",
    )(lat, pos, kern)


def add_parts(tables, feats, part_ref):
    depth = feats[0].shape[1]
    for n in (0, 1):
        total = None
        for pair, feat in zip(tables, feats):
            more = lax.dot_general(pair[n][...], feat[...], (((0,), (0,)), ((), ())), preferred_element_type=jnp.float32)
            total = more if total is None else total + more
        part_ref[:, n * depth:(n + 1) * depth] = total.astype(part_ref.dtype)


def second_kernel(waves, feat_hbm, grid_ref, pos_raw, own_cos, own_sin, mate_feat, pos_ref, cos_ref, sin_ref, part_ref, own_feat, sem, pos_wide):
    fetch = pltpu.make_async_copy(feat_hbm, own_feat, sem)
    fetch.start()
    pos_ref[...] = levels(padded(pos_raw, pos_wide))
    fill_tables(grid_ref[:, :waves // 2], pos_ref, cos_ref, sin_ref)
    fetch.wait()
    add_parts(((own_cos, own_sin), (cos_ref, sin_ref)), (own_feat, mate_feat), part_ref)


def factor_kernel(at, feat_hbm, grid_ref, own_pos, mate_pos, mate_feat, own_cos, own_sin, cos_ref, sin_ref, part_ref, own_feat, sem):
    fetch = pltpu.make_async_copy(feat_hbm, own_feat, sem)
    fetch.start()
    grid = grid_ref[:, at:at + own_cos.shape[1]]
    fill_tables(grid, own_pos, own_cos, own_sin)
    fill_tables(grid, mate_pos, cos_ref, sin_ref)
    fetch.wait()
    add_parts(((own_cos, own_sin), (cos_ref, sin_ref)), (own_feat, mate_feat), part_ref)


def factor_call(kernel, waves, args, rows, depth, outs, kind, scratch=()):
    part = jax.ShapeDtypeStruct((waves // 2, 2 * depth), kind)
    return pl.pallas_call(
        kernel,
        in_specs=[pl.BlockSpec(memory_space=pltpu.HBM)] + [pl.BlockSpec(memory_space=pltpu.VMEM)] * (len(args) - 1),
        out_shape=(*outs, part),
        scratch_shapes=[pltpu.VMEM(args[0].shape, args[0].dtype), pltpu.SemaphoreType.DMA(())] + list(scratch),
        compiler_params=pltpu.CompilerParams(vmem_limit_bytes=12 << 20),
        cost_estimate=pl.CostEstimate(flops=4 * rows * waves * depth, bytes_accessed=8 << 20, transcendentals=0),
    )(*args)


def message_kernel(pieces, sides, has_base, scale, *refs):
    refs = list(refs)
    outs = [refs.pop() for _ in range(sides)][::-1]
    bases = [refs.pop() for _ in range(sides)][::-1] if has_base else None
    rows, depth = outs[0].shape
    tile = min(TILE, rows)
    for side in range(sides):
        def step(t, unused, side=side):
            start = pl.multiple_of(t * tile, tile)
            total = bases[side][pl.ds(start, tile), :] if has_base else None
            for n in range(pieces):
                group = refs[(1 + 2 * sides) * n:(1 + 2 * sides) * (n + 1)]
                for k, at in ((0, 0), (1, depth)):
                    more = jnp.dot(group[1 + 2 * side + k][pl.ds(start, tile), :], group[0][:, at:at + depth], preferred_element_type=jnp.float32)
                    total = more if total is None else total + more
            outs[side][pl.ds(start, tile), :] = (total * scale).astype(outs[side].dtype)
            return unused

        lax.fori_loop(0, rows // tile, step, 0)


def message_part(pieces, bases, scale, kind):
    sides = len(pieces[0][1])
    rows = pieces[0][1][0][0].shape[0]
    depth = pieces[0][0].shape[1] // 2
    args = []
    for filt, tables in pieces:
        args.append(filt)
        for pair in tables:
            args += list(pair)
    if bases is not None:
        args += list(bases)
    waves = sum(p[0].shape[0] for p in pieces)
    return pl.pallas_call(
        functools.partial(message_kernel, len(pieces), sides, bases is not None, scale),
        out_shape=tuple(jax.ShapeDtypeStruct((rows, depth), kind) for _ in range(sides)),
        compiler_params=pltpu.CompilerParams(vmem_limit_bytes=8 << 20),
        cost_estimate=pl.CostEstimate(flops=4 * sides * rows * waves * depth, bytes_accessed=sides * rows * (4 * waves + 4 * depth), transcendentals=0),
    )(*args)


def make_body(groups, wides):
    orders = stage_orders(groups)
    stages = len(orders[0])
    lines = wides // 2
    spots = [(g, w) for g in range(groups) for w in range(wides)]

    def pairs(target):
        out = []
        for g, w in spots:
            tg, tw = target(g, w)
            out.append((g * wides + w, tg * wides + tw))
        return out

    mate = pairs(lambda g, w: (g, w ^ 1))
    hops = [pairs(lambda g, w, j=j: (g ^ (1 << orders[w & 1][j]), w)) for j in range(stages)]
    along = [pairs(lambda g, w, d=d: (g, w ^ (2 * d))) for d in range(lines)]

    def body(features, positions, lattice, kernel):
        waves_all, depth = kernel.shape
        rows = features.shape[0]
        atoms = rows * groups * wides
        inv_atoms = 1.0 / jnp.sqrt(jnp.float32(atoms))
        inv_waves = float(1.0 / waves_all ** 0.5)
        waves = waves_all // (2 * CHUNKS)

        def send_to(x, target):
            return lax.ppermute(x, AXES, target)

        in_hbm = lambda x: pltpu.with_memory_space_constraint(x, pltpu.HBM)
        mate_pos = send_to(positions, mate)
        mate_feat = send_to(features, mate)

        grids, own_levels, own_cos, own_sin, filters = first_part(orders, lines, waves, in_hbm(lattice), in_hbm(positions), in_hbm(kernel))
        block = filters.shape[1]
        if block % 8:
            rows_at = [filter_row(orders, lines, waves_all, waves, c)[0] for c in range(CHUNKS)]
            filters = [lax.dynamic_slice_in_dim(kernel, at, block, 0) for at in rows_at]
        table = table_of(rows, waves)
        mate_levels, cos, sin, part = factor_call(
            functools.partial(second_kernel, waves), waves,
            (in_hbm(features), grids, mate_pos, own_cos, own_sin, mate_feat), rows, depth,
            (jax.ShapeDtypeStruct((32, rows), jnp.bfloat16), table, table), jnp.bfloat16,
            (pltpu.VMEM((8, rows), jnp.float32),))
        tables, parts = {(0, 0): ((own_cos, own_sin), (cos, sin))}, {(0, 0): part}
        for h in (0, 1):
            for c in range(CHUNKS):
                if (c, h) == (0, 0):
                    continue
                own_cos, own_sin, cos, sin, parts[c, h] = factor_call(
                    functools.partial(factor_kernel, c * waves + h * (waves // 2)), waves,
                    (in_hbm(features), grids, own_levels, mate_levels, mate_feat), rows, depth,
                    (table,) * 4, jnp.float32 if h else jnp.bfloat16)
                tables[c, h] = ((own_cos, own_sin), (cos, sin))

        mine = []
        for c in range(CHUNKS):
            send, keep = parts[c, 0], parts[c, 1]
            for j in range(stages):
                got = send_to(send, hops[j])
                keep = keep + got.astype(jnp.float32)
                if j < stages - 1:
                    half = keep.shape[0] // 2
                    send = keep[:half].astype(jnp.bfloat16)
                    keep = keep[half:]
            total = keep[:block]
            outs = [keep[d * block:(d + 1) * block].astype(jnp.bfloat16) for d in range(1, lines)]
            for d in range(1, lines):
                total = total + send_to(outs[d - 1], along[d]).astype(jnp.float32)
            scale = filters[c] * inv_atoms
            mine.append((total * jnp.concatenate([scale, scale], 1)).astype(jnp.bfloat16))

        lasts = []
        for c in range(CHUNKS):
            piece = jnp.concatenate([mine[c]] + [send_to(mine[c], along[d]) for d in range(1, lines)], 0)
            for j in range(stages - 1, 0, -1):
                got = send_to(piece, hops[j])
                piece = jnp.concatenate([got, piece], 0)
            lasts.append((send_to(piece, hops[0]), piece))

        bases = None
        for c in range(CHUNKS):
            pieces = [(lasts[c][1], tables[c, 1])]
            if c > 0:
                pieces.append((lasts[c - 1][0], tables[c - 1, 0]))
            bases = message_part(pieces, bases, 1.0, jnp.float32)
        own, other = tables[CHUNKS - 1, 0]
        away, = message_part([(lasts[-1][0], (other,))], bases[1:], inv_waves, jnp.bfloat16)
        back = send_to(away, mate)
        home, = message_part([(lasts[-1][0], (own,))], bases[:1], inv_waves, jnp.float32)
        return (features.astype(jnp.float32) + (home + back.astype(jnp.float32))).astype(jnp.bfloat16)

    return body


def solution(mesh):
    placed = (P(AXES, None), P(None, AXES), P(), P())
    groups, wides = mesh.shape["grp"], mesh.shape["wide"]
    return jax.shard_map(
        make_body(groups, wides),
        mesh=mesh,
        in_specs=placed,
        out_specs=P(AXES, None),
        check_vma=False,
    )
```

```python
import functools
import jax
import jax.numpy as jnp
from jax import lax
from jax.experimental import pallas as pl
from jax.experimental.pallas import tpu as pltpu
from jax.sharding import PartitionSpec as P


AXES = ("grp", "wide")
CHUNKS = 2
MAGIC = 12582912.0
SIN = (4.4428679, -7.30744342, 3.59478806, -0.78437397)
COS = (1.41420408, -6.97764204, 5.71523826, -1.72834831)
TILE = 256


def turns_to_tables(turns):
    rest = turns - ((turns + MAGIC) - MAGIC)
    square = rest * rest
    half_sin = rest * (SIN[0] + square * (SIN[1] + square * (SIN[2] + square * SIN[3])))
    half_cos = COS[0] + square * (COS[1] + square * (COS[2] + square * COS[3]))
    return 1.0 - half_sin * half_sin, half_sin * half_cos


def stage_orders(groups):
    bits = list(range(groups.bit_length() - 1))
    return bits, bits[::-1]


def stage_bit(orders, j, other=0):
    core = (lax.axis_index("wide") & 1) ^ other
    group = lax.axis_index("grp")
    return ((group >> orders[0][j]) & 1) * (1 - core) + ((group >> orders[1][j]) & 1) * core


def blend(bit, zero, one):
    share = bit.astype(jnp.float32)
    return zero + share * (one - zero)


def padded(ref, wide_ref):
    wide_ref[...] = jnp.zeros_like(wide_ref)
    wide_ref[0:ref.shape[0], :] = ref[...].astype(jnp.float32)
    return wide_ref[...]


def levels(pos):
    parts = []
    for _ in range(3):
        part = pos.astype(jnp.bfloat16).astype(jnp.float32)
        pos = pos - part
        parts.append(part)
    return jnp.concatenate(parts + [jnp.zeros_like(pos)], 0).astype(jnp.bfloat16)


def fill_tile(grid, pos_ref, table_ref, start, tile):
    wide = grid.shape[1]
    turns = lax.dot_general(pos_ref[:, pl.ds(start, tile)], grid, (((0,), (0,)), ((), ())), preferred_element_type=jnp.float32)
    for r in range(0, tile, 32):
        c, s = turns_to_tables(turns[r:r + 32])
        table_ref[pl.ds(start + r, 32), :wide] = c.astype(jnp.bfloat16)
        table_ref[pl.ds(start + r, 32), wide:] = s.astype(jnp.bfloat16)


def fill_table(grid, pos_ref, table_ref):
    rows = table_ref.shape[0]
    tile = min(TILE, rows)

    def fill(t, unused):
        fill_tile(grid, pos_ref, table_ref, pl.multiple_of(t * tile, tile), tile)
        return unused

    lax.fori_loop(0, rows // tile, fill, 0)


def filter_row(orders, lines, waves_all, waves, chunk):
    stages = len(orders[0])
    spot = lax.axis_index("wide") >> 1
    for j in range(stages):
        spot += (1 - stage_bit(orders, j)) * (lines << (stages - 1 - j))
    block = waves // (lines << stages)
    return (lax.axis_index("wide") & 1) * (waves_all // 2) + chunk * waves + spot * block, block


def first_kernel(orders, lines, waves, lat_hbm, pos_hbm, kern_hbm, feat_hbm, grid_ref, own_ref, table_ref, filt_ref, feat_ref, lat_ref, pos_ref, lat_wide, pos_wide, sems):
    pairs = ((lat_hbm, lat_ref), (pos_hbm, pos_ref))
    copies = [pltpu.make_async_copy(a, b, sems.at[n]) for n, (a, b) in enumerate(pairs)]
    for copy in copies:
        copy.start()
    slices = [pltpu.make_async_copy(feat_hbm, feat_ref, sems.at[2 + filt_ref.shape[0]])]
    slices[0].start()
    for c in range(filt_ref.shape[0]):
        at, block = filter_row(orders, lines, kern_hbm.shape[0], waves, c)
        if block % 8 == 0:
            at = pl.multiple_of(at, block)
            slices.append(pltpu.make_async_copy(kern_hbm.at[pl.ds(at, block), :], filt_ref.at[c], sems.at[2 + c]))
            slices[-1].start()
    for copy in copies:
        copy.wait()
    lat = padded(lat_ref, lat_wide)
    side = lat.shape[1] // 2
    line = lax.axis_index("wide") >> 1
    last = side - waves
    for other, first, count, at in ((0, 0, side, 0), (1, last, waves, side)):
        core = (lax.axis_index("wide") & 1) ^ other
        grid = blend(core, lat[:, first:first + count], lat[:, side + first:side + first + count])
        bits = [stage_bit(orders, j, other) for j in range(len(orders[0]))]
        for b in reversed(range(lines.bit_length() - 1)):
            bits.append((line >> b) & 1)
        lane = lax.broadcasted_iota(jnp.int32, grid.shape, 1)
        for j, bit in enumerate(bits):
            step = waves >> (j + 1)
            low = (lane & step) == 0
            swapped = jnp.where(low, pltpu.roll(grid, count - step, 1), pltpu.roll(grid, step, 1))
            grid = blend(bit, grid, swapped)
        grid_ref[:, at:at + count] = jnp.concatenate([grid, grid, grid, jnp.zeros_like(grid)], 0).astype(jnp.bfloat16)
    own_ref[...] = levels(padded(pos_ref, pos_wide))
    fill_table(grid_ref[:, :waves // 2], own_ref, table_ref)
    for copy in slices:
        copy.wait()


def table_of(rows, waves):
    return jax.ShapeDtypeStruct((rows, waves), jnp.bfloat16)


def first_part(orders, lines, waves, lat, pos, kern, feat):
    rows = pos.shape[1]
    block = waves // (lines << len(orders[0]))
    return pl.pallas_call(
        functools.partial(first_kernel, orders, lines, waves),
        in_specs=[pl.BlockSpec(memory_space=pltpu.HBM)] * 4,
        out_shape=(
            jax.ShapeDtypeStruct((32, lat.shape[1] // 2 + waves), jnp.bfloat16),
            jax.ShapeDtypeStruct((32, rows), jnp.bfloat16),
            table_of(rows, waves),
            jax.ShapeDtypeStruct((CHUNKS, block, kern.shape[1]), jnp.float32),
            jax.ShapeDtypeStruct(feat.shape, feat.dtype),
        ),
        scratch_shapes=[
            pltpu.VMEM(lat.shape, lat.dtype),
            pltpu.VMEM(pos.shape, pos.dtype),
            pltpu.VMEM((8, lat.shape[1]), jnp.float32),
            pltpu.VMEM((8, rows), jnp.float32),
            pltpu.SemaphoreType.DMA((3 + CHUNKS,)),
        ],
        compiler_params=pltpu.CompilerParams(vmem_limit_bytes=12 << 20),
        cost_estimate=pl.CostEstimate(flops=rows * waves * 600, bytes_accessed=1 << 20, transcendentals=0),
        name="factor_first",
    )(lat, pos, kern, feat)


def fill_and_add(grid, pos_ref, own_ref, mate_ref, own_feat, mate_feat, part_ref, acc_ref):
    rows, columns = mate_ref.shape
    wide, depth = columns // 2, own_feat.shape[1]
    tile = min(TILE, rows)
    tiles = rows // tile
    width = min(128, wide)
    units = list(range(columns // width))
    split = tiles // 2

    def term(u, table_ref, feat_ref, first, count):
        lhs = table_ref[first:first + count, u * width:(u + 1) * width]
        return lax.dot_general(lhs, feat_ref[first:first + count], (((0,), (0,)), ((), ())), preferred_element_type=jnp.float32)

    def place(u):
        n, row = divmod(u * width, wide)
        return slice(row, row + width), slice(n * depth, (n + 1) * depth)

    jobs = [[] for _ in range(tiles)]
    for t in range(tiles):
        early = t < split or split == 0
        share = max(1, split if early else tiles - split)
        k = t if early else t - split
        jobs[t] = [(early, u) for u in units[k * len(units) // share:(k + 1) * len(units) // share]]
    for t in range(tiles):
        fill_tile(grid, pos_ref, mate_ref, t * tile, tile)
        for early, u in jobs[t]:
            if early:
                acc_ref[place(u)] = term(u, own_ref, own_feat, 0, rows)
            else:
                acc_ref[place(u)] += term(u, mate_ref, mate_feat, 0, split * tile)
    for u in units:
        part_ref[place(u)] = (acc_ref[place(u)] + term(u, mate_ref, mate_feat, split * tile, rows - split * tile)).astype(part_ref.dtype)


def second_kernel(waves, own_feat, grid_ref, pos_raw, own_ref, mate_feat, pos_ref, mate_ref, part_ref, acc_ref, pos_wide):
    pos_ref[...] = levels(padded(pos_raw, pos_wide))
    fill_and_add(grid_ref[:, :waves // 2], pos_ref, own_ref, mate_ref, own_feat, mate_feat, part_ref, acc_ref)


def factor_kernel(at, feat_hbm, grid_ref, own_pos, mate_pos, mate_feat, own_ref, mate_ref, part_ref, own_feat, acc_ref, sem):
    fetch = pltpu.make_async_copy(feat_hbm, own_feat, sem)
    fetch.start()
    grid = grid_ref[:, at:at + own_ref.shape[1] // 2]
    fill_table(grid, own_pos, own_ref)
    fetch.wait()
    fill_and_add(grid, mate_pos, own_ref, mate_ref, own_feat, mate_feat, part_ref, acc_ref)


def factor_call(kernel, waves, args, rows, depth, outs, kind, fetched):
    part = jax.ShapeDtypeStruct((waves // 2, 2 * depth), kind)
    scratch = [pltpu.VMEM(part.shape, jnp.float32)]
    if fetched:
        scratch = [pltpu.VMEM(args[0].shape, args[0].dtype)] + scratch + [pltpu.SemaphoreType.DMA(())]
    else:
        scratch.append(pltpu.VMEM((8, rows), jnp.float32))
    return pl.pallas_call(
        kernel,
        in_specs=[pl.BlockSpec(memory_space=pltpu.HBM if fetched else pltpu.VMEM)] + [pl.BlockSpec(memory_space=pltpu.VMEM)] * (len(args) - 1),
        out_shape=(*outs, part),
        scratch_shapes=scratch,
        compiler_params=pltpu.CompilerParams(vmem_limit_bytes=12 << 20),
        cost_estimate=pl.CostEstimate(flops=4 * rows * waves * depth, bytes_accessed=8 << 20, transcendentals=0),
    )(*args)


def swap_kernel(at, grid_ref, own_pos, table_ref):
    fill_table(grid_ref[:, at:at + table_ref.shape[1] // 2], own_pos, table_ref)


def swap_table(at, waves, grids, own_levels):
    rows = own_levels.shape[1]
    return pl.pallas_call(
        functools.partial(swap_kernel, at),
        out_shape=table_of(rows, waves),
        compiler_params=pltpu.CompilerParams(vmem_limit_bytes=8 << 20),
        cost_estimate=pl.CostEstimate(flops=rows * waves * 600, bytes_accessed=1 << 20, transcendentals=0),
        name="factor_swap",
    )(grids, own_levels)


def final_kernel(scale, table_ref, filt_ref, base_ref, back_ref, feat_ref, out_hbm, out_ref, sems):
    rows, depth = out_ref.shape
    tile = rows // sems.shape[0]
    filt = jnp.concatenate([filt_ref[:, :depth], filt_ref[:, depth:]], 0)
    copies = []
    for t in range(sems.shape[0]):
        at = slice(t * tile, (t + 1) * tile)
        total = base_ref[at] + jnp.dot(table_ref[at], filt, preferred_element_type=jnp.float32)
        total = total * scale + back_ref[at].astype(jnp.float32)
        out_ref[at] = (feat_ref[at].astype(jnp.float32) + total).astype(out_ref.dtype)
        copies.append(pltpu.make_async_copy(out_ref.at[at], out_hbm.at[at], sems.at[t]))
        copies[-1].start()
    for copy in copies:
        copy.wait()


def final_part(table, filt, base, back, feat, scale):
    rows, depth = base.shape
    whole = pl.BlockSpec(memory_space=pltpu.VMEM)
    return pl.pallas_call(
        functools.partial(final_kernel, scale),
        in_specs=[whole] * 5,
        out_specs=pl.BlockSpec(memory_space=pltpu.HBM),
        out_shape=jax.ShapeDtypeStruct((rows, depth), feat.dtype),
        scratch_shapes=[pltpu.VMEM((rows, depth), feat.dtype), pltpu.SemaphoreType.DMA((max(1, rows // TILE),))],
        compiler_params=pltpu.CompilerParams(vmem_limit_bytes=8 << 20),
        cost_estimate=pl.CostEstimate(flops=4 * rows * filt.shape[0] * depth, bytes_accessed=8 << 20, transcendentals=0),
        name="message_final",
    )(table, filt, base, back, feat)


def message_kernel(pieces, sides, has_base, scales, *refs):
    refs = list(refs)
    outs = [refs.pop() for _ in range(sides)][::-1]
    bases = [refs.pop() for _ in range(sides)][::-1] if has_base else None
    rows, depth = outs[0].shape
    tile = min(TILE, rows)
    for side in range(sides):
        def step(t, unused, side=side):
            start = pl.multiple_of(t * tile, tile)
            total = bases[side][pl.ds(start, tile), :] if has_base else None
            for n in range(pieces):
                filt_ref, table_ref = refs[(1 + sides) * n], refs[(1 + sides) * n + 1 + side]
                filt = jnp.concatenate([filt_ref[:, :depth], filt_ref[:, depth:]], 0)
                more = jnp.dot(table_ref[pl.ds(start, tile), :], filt, preferred_element_type=jnp.float32)
                total = more if total is None else total + more
            outs[side][pl.ds(start, tile), :] = (total * scales[side]).astype(outs[side].dtype)
            return unused

        lax.fori_loop(0, rows // tile, step, 0)


def message_part(pieces, bases, scales, kinds):
    sides = len(pieces[0][1])
    rows = pieces[0][1][0].shape[0]
    depth = pieces[0][0].shape[1] // 2
    args = []
    for filt, tables in pieces:
        args += [filt, *tables]
    if bases is not None:
        args += list(bases)
    waves = sum(p[0].shape[0] for p in pieces)
    return pl.pallas_call(
        functools.partial(message_kernel, len(pieces), sides, bases is not None, scales),
        out_shape=tuple(jax.ShapeDtypeStruct((rows, depth), kind) for kind in kinds),
        compiler_params=pltpu.CompilerParams(vmem_limit_bytes=8 << 20),
        cost_estimate=pl.CostEstimate(flops=4 * sides * rows * waves * depth, bytes_accessed=sides * rows * (4 * waves + 4 * depth), transcendentals=0),
    )(*args)


def make_body(groups, wides):
    orders = stage_orders(groups)
    stages = len(orders[0])
    lines = wides // 2
    spots = [(g, w) for g in range(groups) for w in range(wides)]

    def pairs(target):
        out = []
        for g, w in spots:
            tg, tw = target(g, w)
            out.append((g * wides + w, tg * wides + tw))
        return out

    mate = pairs(lambda g, w: (g, w ^ 1))
    hops = [pairs(lambda g, w, j=j: (g ^ (1 << orders[w & 1][j]), w)) for j in range(stages)]
    along = [pairs(lambda g, w, d=d: (g, w ^ (2 * d))) for d in range(lines)]

    def body(features, positions, lattice, kernel):
        waves_all, depth = kernel.shape
        rows = features.shape[0]
        atoms = rows * groups * wides
        inv_atoms = 1.0 / jnp.sqrt(jnp.float32(atoms))
        inv_waves = float(1.0 / waves_all ** 0.5)
        waves = waves_all // (2 * CHUNKS)

        def send_to(x, target):
            return lax.ppermute(x, AXES, target)

        in_hbm = lambda x: pltpu.with_memory_space_constraint(x, pltpu.HBM)
        mate_pos = send_to(positions, mate)
        mate_feat = send_to(features, mate)

        grids, own_levels, own_table, filters, own_feat = first_part(orders, lines, waves, in_hbm(lattice), in_hbm(positions), in_hbm(kernel), in_hbm(features))
        block = filters.shape[1]
        if block % 8:
            rows_at = [filter_row(orders, lines, waves_all, waves, c)[0] for c in range(CHUNKS)]
            filters = [lax.dynamic_slice_in_dim(kernel, at, block, 0) for at in rows_at]
        table = table_of(rows, waves)
        mate_levels, mate_table, part = factor_call(
            functools.partial(second_kernel, waves), waves,
            (own_feat, grids, mate_pos, own_table, mate_feat), rows, depth,
            (jax.ShapeDtypeStruct((32, rows), jnp.bfloat16), table), jnp.bfloat16, False)
        tables, parts = {(0, 0): (own_table, mate_table)}, {(0, 0): part}
        for h in (0, 1):
            for c in range(CHUNKS):
                if (c, h) == (0, 0):
                    continue
                own_table, mate_table, parts[c, h] = factor_call(
                    functools.partial(factor_kernel, c * waves + h * (waves // 2)), waves,
                    (in_hbm(features), grids, own_levels, mate_levels, mate_feat), rows, depth,
                    (table,) * 2, jnp.float32 if h else jnp.bfloat16, True)
                tables[c, h] = (own_table, mate_table)

        mine = []
        for c in range(CHUNKS):
            send, keep = parts[c, 0], parts[c, 1]
            for j in range(stages):
                got = send_to(send, hops[j])
                keep = keep + got.astype(jnp.float32)
                if j < stages - 1:
                    half = keep.shape[0] // 2
                    send = keep[:half].astype(jnp.bfloat16)
                    keep = keep[half:]
                else:
                    outs = [keep[d * block:(d + 1) * block].astype(jnp.bfloat16) for d in range(1, lines)]
                    total = keep[:block]
            gots = [send_to(outs[d - 1], along[d]) for d in range(1, lines)]
            for got in gots:
                total = total + got.astype(jnp.float32)
            scale = filters[c] * inv_atoms
            mine.append((total * jnp.concatenate([scale, scale], 1)).astype(jnp.bfloat16))

        lasts = []
        for c in range(CHUNKS):
            gots = [send_to(mine[c], along[d]) for d in range(1, lines)]
            piece = jnp.concatenate([mine[c]] + gots, 0)
            for j in range(stages - 1, 0, -1):
                got = send_to(piece, hops[j])
                piece = jnp.concatenate([got, piece], 0)
            lasts.append((send_to(piece, hops[0]), piece))

        bases = None
        for c in range(CHUNKS):
            pieces = [(lasts[c][1], tables[c, 1])]
            if c > 0:
                pieces.append((lasts[c - 1][0], tables[c - 1, 0]))
            ends = c == CHUNKS - 1
            bases = message_part(pieces, bases, (1.0, inv_waves if ends else 1.0), (jnp.float32, jnp.bfloat16 if ends else jnp.float32))
        back = send_to(bases[1], mate)
        filt = lasts[-1][0]
        other = send_to(filt, mate)
        base, = message_part([(filt, tables[CHUNKS - 1, 0][:1])], bases[:1], (1.0,), (jnp.float32,))
        swap = swap_table(waves_all // 2, waves, grids, own_levels)
        return final_part(swap, other, base, back, features, inv_waves)

    return body


def solution(mesh):
    placed = (P(AXES, None), P(None, AXES), P(), P())
    groups, wides = mesh.shape["grp"], mesh.shape["wide"]
    return jax.shard_map(
        make_body(groups, wides),
        mesh=mesh,
        in_specs=placed,
        out_specs=P(AXES, None),
        check_vma=False,
    )
```
